32 devices in a mesh: blk: 4 (over x, core), heads: 8 (over z, y).
Axes of the slice: x: 2, y: 2, z: 4, core: 2. Of those that a mesh axis runs over, the one named last changes fastest.
Arguments:
- queries: bfloat16 [2048, 8192], P('blk', 'heads'), may hold values from -6 to 6
- key_rows: bfloat16 [2048, 1024], P('blk'), may hold values from -6 to 6
- value_head_rows: bfloat16 [2048, 1024], P('blk'), may hold values from -6 to 6
- out_weight: bfloat16 [8192, 4096], P('heads', 'blk'), may hold values from -0.0625 to 0.0625
Outputs:
- projected: bfloat16 [2048, 4096], P(('blk', 'heads'))
The draws below stay inside these ranges and needn't reach their ends.
All inputs are finite; a program needn't handle non-finite values.
Results may differ from the reference program's by a relative error of at most 0.013.
Values may be sent and summed in bfloat16 or wider, within the bound.
A program may use at most 64 MiB of HBM per device.

```python
import jax
import jax.numpy as jnp
from jax import lax

QUERY_HEADS = 64
KEY_VALUE_HEADS = 8
HEAD_SIZE = 128
DOUT = 4096
SEQUENCE_TOKENS = 2048
HPD = 8
N_HEADS = 8


def draw_queries(key, part):
    random_subkey = jax.random.fold_in(key, 11)
    value_entries = jnp.clip(jax.random.normal(random_subkey, (SEQUENCE_TOKENS, QUERY_HEADS * HEAD_SIZE), jnp.float32) * 1.41, -6.0, 6.0)
    return value_entries.astype(jnp.bfloat16)


def draw_key_rows(key, part):
    random_subkey = jax.random.fold_in(key, 12)
    value_entries = jnp.clip(jax.random.normal(random_subkey, (SEQUENCE_TOKENS, KEY_VALUE_HEADS * HEAD_SIZE), jnp.float32) * 1.41, -6.0, 6.0)
    return value_entries.astype(jnp.bfloat16)


def level_of(rng, dims, shards, smallest, top_value):
    loudness, own = 1.0, jax.random.fold_in(rng, 6)
    for position, blocks in shards:
        heights = jnp.exp(jax.random.uniform(jax.random.fold_in(own, position), (blocks,), jnp.float32, smallest / len(shards), top_value / len(shards)))
        loudness = loudness * jnp.repeat(heights, dims[position] // blocks).reshape([-1 if axis == position else 1 for axis in range(len(dims))])
    return loudness


def noise(stream_key, dims, width, most, cuts=(), held_as=jnp.bfloat16):
    values = jax.random.normal(stream_key, dims, jnp.float32) * width
    if len(cuts) > 0:
        values = level_of(stream_key, dims, cuts, -0.22, 0.18) * values
    return jnp.clip(values, min=-most, max=most).astype(held_as)


def setup_inputs(seed: int = 0) -> dict:
    key_list = jax.random.split(jax.random.key(seed), 5)
    return {
        "queries": draw_queries(jax.random.fold_in(key_list[4], 71), 0),
        "key_rows": draw_key_rows(jax.random.fold_in(key_list[4], 71), 0),
        "value_head_rows": noise(key_list[2], (SEQUENCE_TOKENS, KEY_VALUE_HEADS * HEAD_SIZE), 1.0, 6.0, ((0, 4),)),
        "out_weight": noise(key_list[3], (QUERY_HEADS * HEAD_SIZE, DOUT), (QUERY_HEADS * HEAD_SIZE) ** -0.5, 0.0625, ((0, 8), (1, 4))),
    }


def reference(queries, key_rows, value_head_rows, out_weight):
    group_width = QUERY_HEADS // KEY_VALUE_HEADS
    inv_root = HEAD_SIZE ** -0.5
    positions = jnp.arange(SEQUENCE_TOKENS, dtype=jnp.int32)
    visible = positions[:, None] >= positions[None, :]

    def one_head(head_number):
        query_cols = lax.dynamic_slice_in_dim(queries, head_number * HEAD_SIZE, HEAD_SIZE, 1)
        shared = (head_number // group_width) * HEAD_SIZE
        key_cols = lax.dynamic_slice_in_dim(key_rows, shared, HEAD_SIZE, 1)
        value_cols = lax.dynamic_slice_in_dim(value_head_rows, shared, HEAD_SIZE, 1)
        scores = jnp.dot(query_cols, key_cols.T, preferred_element_type=jnp.float32) * inv_root
        masked = jnp.where(visible, scores, -jnp.inf)
        row_max = jnp.max(masked, axis=1, keepdims=True)
        weights = jnp.where(visible, jnp.exp(masked - row_max), 0.0)
        totals = jnp.sum(weights, axis=1, keepdims=True)
        mixed = jnp.dot(weights.astype(jnp.bfloat16), value_cols, preferred_element_type=jnp.float32)
        return (mixed / totals).astype(jnp.bfloat16)

    heads_out = lax.map(one_head, jnp.arange(QUERY_HEADS, dtype=jnp.int32))
    attention = heads_out.transpose(1, 0, 2).reshape(SEQUENCE_TOKENS, QUERY_HEADS * HEAD_SIZE)
    span = HPD * HEAD_SIZE

    def add_group(running, group_number):
        features = lax.dynamic_slice_in_dim(attention, group_number * span, span, 1)
        weight_rows = lax.dynamic_slice_in_dim(out_weight, group_number * span, span, 0)
        partial_value = jnp.dot(features, weight_rows, preferred_element_type=jnp.float32).astype(jnp.bfloat16)
        return running + partial_value.astype(jnp.float32), None

    running, _ = lax.scan(add_group, jnp.zeros((SEQUENCE_TOKENS, DOUT), jnp.float32), jnp.arange(N_HEADS, dtype=jnp.int32))
    return running.astype(jnp.bfloat16)
```

```python
import functools
import math

import jax
import jax.numpy as jnp
from jax import lax
from jax.experimental import pallas as pl
from jax.experimental.pallas import tpu as pltpu
from jax.sharding import PartitionSpec as P

QUERY_HEADS = 64
KEY_VALUE_HEADS = 8
HEAD_SIZE = 128
MASKED_SCORE = -1e30
COLUMN_STEP = 256
TOTAL_ROWS = 16
LAG = 2
LAST = 8
KEY_TILE = 256
F32 = jnp.float32
BF16 = jnp.bfloat16


def kernel(nb, nh, q_hbm, k_ref, v_ref, w_ref, out_ref,
           q_ref, kbuf, vbuf, vturn, wbuf, sbuf, mbuf, acc, top, att, ysend, yrecv, psend, precv, kept, zsend, zrecv,
           local_sem, kv_send, kv_recv, relay_send, w_send, w_recv,
           att_send, att_recv, y_send, y_recv, p_send, p_recv, z_send, z_recv):
    nx, nz = nb // 2, nh // 2
    rows = k_ref.shape[0]
    piece = rows // nh
    half, quarter = rows // 2, rows // 4
    pairs = nz // 2
    heads = q_ref.shape[4] // HEAD_SIZE
    wcols = w_ref.shape[1]
    step = wbuf.shape[2]
    per = wcols // step
    ns = 2 * per
    scale = math.log2(math.e) * HEAD_SIZE ** (-0.5)

    b, h = lax.axis_index("blk"), lax.axis_index("heads")
    x, c = b // 2, b % 2
    z, y = h // 2, h % 2
    odd, seat = z % 2, z // 2
    partner = x * 2 + (1 - c)
    kv_col = pl.multiple_of((h * heads // (QUERY_HEADS // KEY_VALUE_HEADS)) * HEAD_SIZE, HEAD_SIZE)

    def remote(src, dst, ssem, rsem, blk, hd):
        return pltpu.make_async_remote_copy(
            src_ref=src, dst_ref=dst, send_sem=ssem, recv_sem=rsem,
            device_id=(blk, hd), device_id_type=pl.DeviceIdType.MESH)

    k_own = k_ref.at[:, pl.ds(kv_col, HEAD_SIZE)]
    v_own = v_ref.at[:, pl.ds(kv_col, HEAD_SIZE)]
    local_k = pltpu.make_async_copy(k_own, kbuf.at[b], local_sem.at[0])
    local_v = pltpu.make_async_copy(v_own, vbuf.at[b], local_sem.at[1])
    local_k.start()
    local_v.start()

    def group_y(g):
        return jnp.where(g == 0, 1 - y, y)

    def group_odd(u):
        return (1 - odd) if u == 0 else odd

    local_q = [pltpu.make_async_copy(q_hbm.at[:, group_odd(u), group_y(g)], q_ref.at[g, u], local_sem.at[2 + 2 * g + u])
               for g in range(2) for u in range(2)]
    for copy in local_q:
        copy.start()

    def w_cols(s):
        return w_ref.at[:, pl.ds(s * step, step)]

    local_w = [pltpu.make_async_copy(w_cols(s), wbuf.at[c * per + s], local_sem.at[6 + s]) for s in range(per)]
    for copy in local_w:
        copy.start()

    barrier = pltpu.get_barrier_semaphore()

    def greet(blk, hd):
        pl.semaphore_signal(barrier, inc=1, device_id=(blk, hd), device_id_type=pl.DeviceIdType.MESH)

    z_pair = (z + 1 - 2 * odd) * 2 + y
    y_pair = z * 2 + (1 - y)

    def owner(m):
        return (2 * m + odd) * 2 + y

    greet(partner, h)
    greet(b, y_pair)
    greet(b, z_pair)
    for j in range(nx):
        for m in range(pairs):
            @pl.when(jnp.logical_or(j != x, m != seat))
            def _():
                greet(j * 2 + c, owner(m))
    pl.semaphore_wait(barrier, 3 + nx * pairs - 1)

    kv = ((kbuf, k_own), (vbuf, v_own))

    def kv_copy(buf, own, n, src_blk, dst_blk, ssem):
        return remote(own, buf.at[src_blk], ssem, kv_recv.at[n, src_blk], dst_blk, h)

    @pl.when(c == 0)
    def _():
        for n, (buf, own) in enumerate(kv):
            kv_copy(buf, own, n, b, partner, kv_send.at[n, nx]).start()

    def kv_forward():
        for j in range(1, nx):
            @pl.when(j > x)
            def _():
                for n, (buf, own) in enumerate(kv):
                    kv_copy(buf, own, n, b, j * 2 + c, kv_send.at[n, j]).start()

    pl.when(c == 1)(kv_forward)

    def w_copy(s, side):
        return remote(w_cols(s), wbuf.at[side * per + s], w_send.at[s], w_recv.at[s], partner, h)

    for s in range(per):
        w_copy(s, c).start()

    def turn(j):
        vturn[j, :HEAD_SIZE] = vbuf[j].T
        vturn[j, HEAD_SIZE:] = jnp.ones((TOTAL_ROWS, rows), BF16)

    tile = sbuf.shape[2]
    tiles = rows // tile

    def score_tile(g, hd, j, t, own):
        cols = pl.ds(pl.multiple_of(hd * HEAD_SIZE, HEAD_SIZE), HEAD_SIZE)
        q = q_ref[g, :, :, :, cols].reshape(half, HEAD_SIZE)
        k = kbuf[j, t * tile:(t + 1) * tile]
        s = lax.dot_general(k, q, (((1,), (1,)), ((), ())), preferred_element_type=F32) * scale
        if own:
            row = lax.broadcasted_iota(jnp.int32, (tile, half), 1)
            chip = row % quarter // piece * 2 + jnp.where(row < quarter, 1 - odd, odd)
            position = (chip * 2 + group_y(g)) * piece + row % piece
            visible = position >= lax.broadcasted_iota(jnp.int32, (tile, half), 0) + t * tile
            s = jnp.where(visible, s, MASKED_SCORE)
        return s

    def block(g, j, own):
        def put(hd, slot, t, m):
            s = score_tile(g, hd, j, t, own)
            sbuf[slot, t] = s
            n = jnp.max(s, axis=0, keepdims=True)
            return n if m is None else jnp.maximum(m, n)

        def step(hd, following, slot):
            m = mbuf[slot][:1]
            if not own:
                old = top[g, hd][:1]
                m = jnp.maximum(old, m)
            mixed, ahead = None, None
            for t in range(tiles):
                ahead = put(following, 1 - slot, t, ahead)
                p = jnp.exp2(sbuf[slot, t] - m).astype(BF16)
                d = jnp.dot(vturn[j, :, t * tile:(t + 1) * tile], p, preferred_element_type=F32)
                mixed = d if mixed is None else mixed + d
            mbuf[1 - slot] = jnp.broadcast_to(ahead, (8, half))
            if not own:
                mixed += acc[g, hd] * jnp.exp2(old - m)
            acc[g, hd] = mixed
            top[g, hd] = jnp.broadcast_to(m, (8, half))

        ahead = None
        for t in range(tiles):
            ahead = put(0, 0, t, ahead)
        mbuf[0] = jnp.broadcast_to(ahead, (8, half))

        def pair(i, carry):
            step(2 * i, 2 * i + 1, 0)
            step(2 * i + 1, jnp.minimum(2 * i + 2, heads - 1), 1)
            return carry

        lax.fori_loop(0, heads // 2, pair, 0)

    def side(g, core):
        def one(i, carry):
            block(g, 2 * (x - 1 - i) + core, False)
            return carry

        lax.fori_loop(0, x, one, 0)

    def earlier(g):
        def one(i, carry):
            block(g, b - 1 - i, False)
            return carry

        lax.fori_loop(0, b, one, 0)

    def diagonal(start, stop):
        def one(g, carry):
            block(g, b, True)
            return carry

        lax.fori_loop(start, stop, one, 0)

    def att_copy(g, i, src):
        return remote(att.at[src, g], att.at[src, g], att_send.at[g, i], att_recv.at[g, src],
                      lax.rem(x + i, nx) * 2 + c, h)

    def finish(g):
        def one(hd, carry):
            cols = pl.ds(pl.multiple_of(hd * HEAD_SIZE, HEAD_SIZE), HEAD_SIZE)
            a = acc[g, hd]
            mixed = (a[:HEAD_SIZE] / a[HEAD_SIZE:HEAD_SIZE + 1]).T.astype(BF16)
            att[x, g, :, :, cols] = mixed.reshape(2, quarter, HEAD_SIZE)
            return carry

        lax.fori_loop(0, heads, one, 0)
        for i in range(1, nx):
            att_copy(g, i, x).start()

    def wait_partner():
        @pl.when(c == 1)
        def _():
            for n, (buf, own) in enumerate(kv):
                kv_copy(buf, own, n, b - 1, partner, kv_send.at[n, nx]).wait_recv()
            turn(b - 1)

    def arrive(core):
        for j in range(nx - 1):
            @pl.when(j < x)
            def _():
                at = j * 2 + core
                for n, (buf, own) in enumerate(kv):
                    kv_copy(buf, own, n, at, partner, kv_send.at[n, 0]).wait_recv()

                @pl.when(c == core)
                def _():
                    for n, (buf, own) in enumerate(kv):
                        kv_copy(buf, buf.at[at], n, at, partner, relay_send.at[n, j]).start()

                turn(at)

    def chip(i):
        return x if i == 0 else lax.rem(x + i, nx)

    def along_y(s):
        return s < ns - ns // 4

    def y_copy(i, s):
        return remote(ysend.at[i, s], yrecv.at[i, s], y_send.at[i, s], y_recv.at[i, s], b, y_pair if along_y(s) else z_pair)

    def p_copy(i, s):
        return remote(psend.at[i, s], precv.at[i, s], p_send.at[i, s], p_recv.at[i, s], b, z_pair if along_y(s) else y_pair)

    def z_copy(i, s, m):
        return remote(zsend.at[i, s, m], zrecv.at[x, s, seat], z_send.at[i, s, m], z_recv.at[x, s, seat],
                      chip(i) * 2 + c, owner(m))

    def z_each(i, body):
        for m in range(pairs):
            if i == 0:
                pl.when(m != seat)(functools.partial(body, m))
            else:
                body(m)

    def project(i, s, far):
        a = att[chip(i), far] if along_y(s) else att[chip(i), :, far]
        return jnp.dot(a.reshape(half, a.shape[-1]), wbuf[s], preferred_element_type=F32)

    def first(i, s):
        ysend[i, s] = project(i, s, 0).astype(BF16)
        y_copy(i, s).start()

    def second(i, s):
        d = project(i, s, 1)
        y_copy(i, s).wait_recv()
        d += yrecv[i, s].astype(F32)
        psend[i, s] = d[:quarter].astype(BF16)
        p_copy(i, s).start()
        kept[i, s] = d[quarter:]

    def third(i, s):
        p_copy(i, s).wait_recv()
        d = (kept[i, s] + precv[i, s].astype(F32)).astype(BF16)
        zsend[i, s] = d.reshape(pairs, piece, step)
        z_each(i, lambda m: z_copy(i, s, m).start())
        if i == 0:
            zrecv[x, s, seat] = zsend[i, s, seat]

    def fourth(i, s):
        src = x if i == 0 else lax.rem(x + nx - i, nx)

        def arrived(m):
            remote(zsend.at[0, s, m], zrecv.at[src, s, m], z_send.at[0, s, m], z_recv.at[src, s, m], b, y_pair).wait_recv()

        z_each(i, arrived)
        total = zrecv[src, s, 0].astype(F32)
        for m in range(1, pairs):
            total += zrecv[src, s, m].astype(F32)
        col = pl.multiple_of((src * ns + s) * step, step)
        out_ref[:, pl.ds(col, step)] = total.astype(BF16)

    def landed(g, i):
        att_copy(g, i, chip(i)).wait_recv()

    local_k.wait()
    local_v.wait()
    turn(b)
    for copy in local_q:
        copy.wait()
    ready = jnp.where(jnp.logical_and(x > 0, c == 0), 2, 1)
    diagonal(0, ready)
    pl.when(c == 0)(kv_forward)
    wait_partner()

    @pl.when(c == 1)
    def _():
        block(0, b - 1, False)

    for core in (1, 0):
        arrive(core)
        side(0, core)
    finish(0)
    for s in range(per):
        local_w[s].wait()
    for s in range(per):
        w_copy(s, 1 - c).wait_recv()

    along = [s for s in range(ns) if along_y(s)]
    across = [s for s in range(ns) if not along_y(s)]
    done = []

    def advance(i, s):
        second(i, s)
        done.append((i, s))
        if len(done) > LAG:
            third(*done[-1 - LAG])
        if len(done) > LAST:
            fourth(*done[-1 - LAST])

    for s in along:
        first(0, s)
    diagonal(ready, 2)
    earlier(1)
    finish(1)
    for s in across:
        first(0, s)
    cut = (len(along) + 1) // 2
    for s in along[:cut] + across:
        advance(0, s)
    for i in range(1, nx):
        landed(0, i)
        for s in along[:cut]:
            first(i, s)
        for s in along[cut:]:
            advance(i - 1, s)
        landed(1, i)
        for s in across + along[cut:cut + 1]:
            first(i, s)
        for s in along[:cut - 1] + across:
            advance(i, s)
        for s in along[cut + 1:]:
            first(i, s)
        for s in along[cut - 1:cut]:
            advance(i, s)
    for s in along[cut:]:
        advance(nx - 1, s)
    for chunk in done[-LAG:]:
        third(*chunk)
    for chunk in done[-LAST:]:
        fourth(*chunk)

    @pl.when(c == 0)
    def _():
        for n, (buf, own) in enumerate(kv):
            kv_copy(buf, own, n, b, partner, kv_send.at[n, nx]).wait_send()

    for j in range(1, nx):
        @pl.when(j > x)
        def _():
            for n, (buf, own) in enumerate(kv):
                kv_copy(buf, own, n, b, j * 2 + c, kv_send.at[n, j]).wait_send()

    for j in range(nx - 1):
        @pl.when(j < x)
        def _():
            for n, (buf, own) in enumerate(kv):
                at = j * 2 + c
                kv_copy(buf, buf.at[at], n, at, partner, relay_send.at[n, j]).wait_send()

    for s in range(per):
        w_copy(s, c).wait_send()
    for g in range(2):
        for i in range(1, nx):
            att_copy(g, i, x).wait_send()

    for i in range(nx):
        for s in range(ns):
            y_copy(i, s).wait_send()
            p_copy(i, s).wait_send()
            z_each(i, lambda m: z_copy(i, s, m).wait_send())


def shards(nb, nh, queries, key_rows, value_head_rows, out_weight):
    rows, qcols = queries.shape
    depth, wcols = out_weight.shape
    heads = qcols // HEAD_SIZE
    nx, nz = nb // 2, nh // 2
    pairs = nz // 2
    piece, half, quarter = rows // nh, rows // 2, rows // 4
    step = math.gcd(wcols, COLUMN_STEP)
    ns = 2 * wcols // step
    tile = math.gcd(rows, KEY_TILE)
    q = queries.reshape(pairs, 2, 2, piece, qcols)
    dma = pltpu.SemaphoreType.DMA
    vmem = pl.BlockSpec(memory_space=pltpu.VMEM)
    hbm = pl.BlockSpec(memory_space=pl.ANY)
    return pl.pallas_call(
        functools.partial(kernel, nb, nh),
        out_shape=jax.ShapeDtypeStruct((piece, wcols * nb), BF16),
        in_specs=[hbm, hbm, hbm, hbm],
        out_specs=vmem,
        scratch_shapes=[
            pltpu.VMEM((2, 2, pairs, piece, qcols), BF16),
            pltpu.VMEM((nb, rows, HEAD_SIZE), BF16),
            pltpu.VMEM((nb, rows, HEAD_SIZE), BF16),
            pltpu.VMEM((nb, HEAD_SIZE + TOTAL_ROWS, rows), BF16),
            pltpu.VMEM((ns, depth, step), BF16),
            pltpu.VMEM((2, rows // tile, tile, half), F32),
            pltpu.VMEM((2, 8, half), F32),
            pltpu.VMEM((2, heads, HEAD_SIZE + TOTAL_ROWS, half), F32),
            pltpu.VMEM((2, heads, 8, half), F32),
            pltpu.VMEM((nx, 2, 2, quarter, qcols), BF16),
            pltpu.VMEM((nx, ns, half, step), BF16),
            pltpu.VMEM((nx, ns, half, step), BF16),
            pltpu.VMEM((nx, ns, quarter, step), BF16),
            pltpu.VMEM((nx, ns, quarter, step), BF16),
            pltpu.VMEM((nx, ns, quarter, step), F32),
            pltpu.VMEM((nx, ns, pairs, piece, step), BF16),
            pltpu.VMEM((nx, ns, pairs, piece, step), BF16),
            dma((6 + ns // 2,)),
            dma((2, nx + 1)),
            dma((2, nb)),
            dma((2, nx)),
            dma((ns // 2,)),
            dma((ns // 2,)),
            dma((2, nx)),
            dma((2, nx)),
            dma((nx, ns)),
            dma((nx, ns)),
            dma((nx, ns)),
            dma((nx, ns)),
            dma((nx, ns, pairs)),
            dma((nx, ns, pairs)),
        ],
        compiler_params=pltpu.CompilerParams(
            collective_id=0, has_side_effects=True, vmem_limit_bytes=66_000_000),
    )(q, key_rows, value_head_rows, out_weight)


def solution(mesh):
    in_specs = (P("blk", "heads"), P("blk", None), P("blk", None), P("heads", "blk"))
    out_specs = P(("blk", "heads"), None)
    body = functools.partial(shards, mesh.shape["blk"], mesh.shape["heads"])
    return jax.shard_map(body, mesh=mesh, in_specs=in_specs, out_specs=out_specs, check_vma=False)
```

```python
import functools
import math

import jax
import jax.numpy as jnp
from jax import lax
from jax.experimental import pallas as pl
from jax.experimental.pallas import tpu as pltpu
from jax.sharding import PartitionSpec as P

QUERY_HEADS = 64
KEY_VALUE_HEADS = 8
HEAD_SIZE = 128
MASKED_SCORE = -1e30
COLUMN_STEP = 256
TOTAL_ROWS = 16
LAG = 4
LAST = 9
KEY_TILE = 256
F32 = jnp.float32
BF16 = jnp.bfloat16


def kernel(nb, nh, q_hbm, k_ref, v_ref, w_ref, out_ref,
           q_ref, kbuf, vbuf, vturn, wbuf, sbuf, mbuf, acc, top, att, ysend, yrecv, psend, precv, kept, zsend, zrecv,
           local_sem, kv_send, kv_recv, relay_send, w_send, w_recv,
           att_send, att_recv, y_send, y_recv, p_send, p_recv, z_send, z_recv):
    nx, nz = nb // 2, nh // 2
    rows = k_ref.shape[0]
    piece = rows // nh
    half, quarter = rows // 2, rows // 4
    pairs = nz // 2
    heads = q_ref.shape[4] // HEAD_SIZE
    wcols = w_ref.shape[1]
    step = wbuf.shape[2]
    per = wcols // step
    ns = 2 * per
    scale = math.log2(math.e) * HEAD_SIZE ** (-0.5)

    b, h = lax.axis_index("blk"), lax.axis_index("heads")
    x, c = b // 2, b % 2
    z, y = h // 2, h % 2
    odd, seat = z % 2, z // 2
    partner = x * 2 + (1 - c)
    kv_col = pl.multiple_of((h * heads // (QUERY_HEADS // KEY_VALUE_HEADS)) * HEAD_SIZE, HEAD_SIZE)

    def remote(src, dst, ssem, rsem, blk, hd):
        return pltpu.make_async_remote_copy(
            src_ref=src, dst_ref=dst, send_sem=ssem, recv_sem=rsem,
            device_id=(blk, hd), device_id_type=pl.DeviceIdType.MESH)

    k_own = k_ref.at[:, pl.ds(kv_col, HEAD_SIZE)]
    v_own = v_ref.at[:, pl.ds(kv_col, HEAD_SIZE)]
    local_k = pltpu.make_async_copy(k_own, kbuf.at[b], local_sem.at[0])
    local_v = pltpu.make_async_copy(v_own, vbuf.at[b], local_sem.at[1])
    local_k.start()
    local_v.start()

    def group_y(g):
        return jnp.where(g == 0, 1 - y, y)

    def group_odd(u):
        return (1 - odd) if u == 0 else odd

    local_q = [pltpu.make_async_copy(q_hbm.at[:, group_odd(u), group_y(g)], q_ref.at[g, u], local_sem.at[2 + 2 * g + u])
               for g in range(2) for u in range(2)]
    for copy in local_q:
        copy.start()

    def w_cols(s):
        return w_ref.at[:, pl.ds(s * step, step)]

    local_w = [pltpu.make_async_copy(w_cols(s), wbuf.at[c * per + s], local_sem.at[6 + s]) for s in range(per)]
    for copy in local_w:
        copy.start()

    barrier = pltpu.get_barrier_semaphore()

    def greet(blk, hd):
        pl.semaphore_signal(barrier, inc=1, device_id=(blk, hd), device_id_type=pl.DeviceIdType.MESH)

    z_pair = (z + 1 - 2 * odd) * 2 + y
    y_pair = z * 2 + (1 - y)

    def owner(m):
        return (2 * m + odd) * 2 + y

    greet(partner, h)
    greet(b, y_pair)
    greet(b, z_pair)
    for j in range(nx):
        for m in range(pairs):
            @pl.when(jnp.logical_or(j != x, m != seat))
            def _():
                greet(j * 2 + c, owner(m))
    pl.semaphore_wait(barrier, 3 + nx * pairs - 1)

    kv = ((kbuf, k_own), (vbuf, v_own))

    def kv_copy(buf, own, n, src_blk, dst_blk, ssem):
        return remote(own, buf.at[src_blk], ssem, kv_recv.at[n, src_blk], dst_blk, h)

    @pl.when(c == 0)
    def _():
        for n, (buf, own) in enumerate(kv):
            kv_copy(buf, own, n, b, partner, kv_send.at[n, nx]).start()

    def kv_forward():
        for j in range(1, nx):
            @pl.when(j > x)
            def _():
                for n, (buf, own) in enumerate(kv):
                    kv_copy(buf, own, n, b, j * 2 + c, kv_send.at[n, j]).start()

    pl.when(c == 1)(kv_forward)

    def w_copy(s, side):
        return remote(w_cols(s), wbuf.at[side * per + s], w_send.at[s], w_recv.at[s], partner, h)

    for s in range(per):
        w_copy(s, c).start()

    def turn(j):
        vturn[j, :HEAD_SIZE] = vbuf[j].T
        vturn[j, HEAD_SIZE:] = jnp.ones((TOTAL_ROWS, rows), BF16)

    tile = sbuf.shape[2]
    tiles = rows // tile

    def score_tile(g, hd, j, t, own):
        cols = pl.ds(pl.multiple_of(hd * HEAD_SIZE, HEAD_SIZE), HEAD_SIZE)
        q = q_ref[g, :, :, :, cols].reshape(half, HEAD_SIZE)
        k = kbuf[j, t * tile:(t + 1) * tile]
        s = lax.dot_general(k, q, (((1,), (1,)), ((), ())), preferred_element_type=F32) * scale
        if own:
            row = lax.broadcasted_iota(jnp.int32, (tile, half), 1)
            chip = row % quarter // piece * 2 + jnp.where(row < quarter, 1 - odd, odd)
            position = (chip * 2 + group_y(g)) * piece + row % piece
            visible = position >= lax.broadcasted_iota(jnp.int32, (tile, half), 0) + t * tile
            s = jnp.where(visible, s, MASKED_SCORE)
        return s

    def block(g, j, own):
        def put(hd, slot, t, m):
            s = score_tile(g, hd, j, t, own)
            sbuf[slot, t] = s
            n = jnp.max(s, axis=0, keepdims=True)
            return n if m is None else jnp.maximum(m, n)

        def step(hd, following, slot):
            m = mbuf[slot][:1]
            if not own:
                old = top[g, hd][:1]
                m = jnp.maximum(old, m)
            mixed, ahead = None, None
            for t in range(tiles):
                ahead = put(following, 1 - slot, t, ahead)
                p = jnp.exp2(sbuf[slot, t] - m).astype(BF16)
                d = jnp.dot(vturn[j, :, t * tile:(t + 1) * tile], p, preferred_element_type=F32)
                mixed = d if mixed is None else mixed + d
            mbuf[1 - slot] = jnp.broadcast_to(ahead, (8, half))
            if not own:
                mixed += acc[g, hd] * jnp.exp2(old - m)
            acc[g, hd] = mixed
            top[g, hd] = jnp.broadcast_to(m, (8, half))

        ahead = None
        for t in range(tiles):
            ahead = put(0, 0, t, ahead)
        mbuf[0] = jnp.broadcast_to(ahead, (8, half))

        def pair(i, carry):
            step(2 * i, 2 * i + 1, 0)
            step(2 * i + 1, jnp.minimum(2 * i + 2, heads - 1), 1)
            return carry

        lax.fori_loop(0, heads // 2, pair, 0, unroll=True)

    def side(g, core):
        def one(i, carry):
            block(g, 2 * (x - 1 - i) + core, False)
            return carry

        lax.fori_loop(0, x, one, 0)

    def earlier(g):
        def one(i, carry):
            block(g, b - 1 - i, False)
            return carry

        lax.fori_loop(0, b, one, 0)

    def diagonal(start, stop):
        def one(g, carry):
            block(g, b, True)
            return carry

        lax.fori_loop(start, stop, one, 0)

    def att_copy(g, i, src):
        return remote(att.at[src, g], att.at[src, g], att_send.at[g, i], att_recv.at[g, src],
                      lax.rem(x + i, nx) * 2 + c, h)

    def finish(g):
        def one(hd, carry):
            cols = pl.ds(pl.multiple_of(hd * HEAD_SIZE, HEAD_SIZE), HEAD_SIZE)
            a = acc[g, hd]
            mixed = (a[:HEAD_SIZE] / a[HEAD_SIZE:HEAD_SIZE + 1]).T.astype(BF16)
            att[x, g, :, :, cols] = mixed.reshape(2, quarter, HEAD_SIZE)
            return carry

        lax.fori_loop(0, heads, one, 0, unroll=True)
        for i in range(1, nx):
            att_copy(g, i, x).start()

    def wait_partner():
        @pl.when(c == 1)
        def _():
            for n, (buf, own) in enumerate(kv):
                kv_copy(buf, own, n, b - 1, partner, kv_send.at[n, nx]).wait_recv()
            turn(b - 1)

    def arrive(core):
        for j in range(nx - 1):
            @pl.when(j < x)
            def _():
                at = j * 2 + core
                for n, (buf, own) in enumerate(kv):
                    kv_copy(buf, own, n, at, partner, kv_send.at[n, 0]).wait_recv()

                @pl.when(c == core)
                def _():
                    for n, (buf, own) in enumerate(kv):
                        kv_copy(buf, buf.at[at], n, at, partner, relay_send.at[n, j]).start()

                turn(at)

    def chip(i):
        return x if i == 0 else lax.rem(x + i, nx)

    def along_y(s):
        return s < ns - ns // 4

    def y_copy(i, s):
        return remote(ysend.at[i, s], yrecv.at[i, s], y_send.at[i, s], y_recv.at[i, s], b, y_pair if along_y(s) else z_pair)

    def p_copy(i, s):
        return remote(psend.at[i, s], precv.at[i, s], p_send.at[i, s], p_recv.at[i, s], b, z_pair if along_y(s) else y_pair)

    def z_copy(i, s, m):
        return remote(zsend.at[i, s, m], zrecv.at[x, s, seat], z_send.at[i, s, m], z_recv.at[x, s, seat],
                      chip(i) * 2 + c, owner(m))

    def z_each(i, body):
        for m in range(pairs):
            if i == 0:
                pl.when(m != seat)(functools.partial(body, m))
            else:
                body(m)

    def project(i, s, far):
        a = att[chip(i), far] if along_y(s) else att[chip(i), :, far]
        return jnp.dot(a.reshape(half, a.shape[-1]), wbuf[s], preferred_element_type=F32)

    def first(i, s):
        ysend[i, s] = project(i, s, 0).astype(BF16)
        y_copy(i, s).start()

    def second(i, s):
        d = project(i, s, 1)
        y_copy(i, s).wait_recv()
        d += yrecv[i, s].astype(F32)
        psend[i, s] = d[:quarter].astype(BF16)
        p_copy(i, s).start()
        kept[i, s] = d[quarter:]

    def third(i, s):
        p_copy(i, s).wait_recv()
        d = (kept[i, s] + precv[i, s].astype(F32)).astype(BF16)
        zsend[i, s] = d.reshape(pairs, piece, step)
        z_each(i, lambda m: z_copy(i, s, m).start())
        if i == 0:
            zrecv[x, s, seat] = zsend[i, s, seat]

    def fourth(i, s):
        src = x if i == 0 else lax.rem(x + nx - i, nx)

        def arrived(m):
            remote(zsend.at[0, s, m], zrecv.at[src, s, m], z_send.at[0, s, m], z_recv.at[src, s, m], b, y_pair).wait_recv()

        z_each(i, arrived)
        total = zrecv[src, s, 0].astype(F32)
        for m in range(1, pairs):
            total += zrecv[src, s, m].astype(F32)
        col = pl.multiple_of((src * ns + s) * step, step)
        out_ref[:, pl.ds(col, step)] = total.astype(BF16)

    def landed(g, i):
        att_copy(g, i, chip(i)).wait_recv()

    local_k.wait()
    local_v.wait()
    turn(b)
    for copy in local_q:
        copy.wait()
    ready = jnp.where(jnp.logical_and(x > 0, c == 0), 2, 1)
    diagonal(0, ready)
    pl.when(c == 0)(kv_forward)
    wait_partner()

    @pl.when(c == 1)
    def _():
        block(0, b - 1, False)

    for core in (1, 0):
        arrive(core)
        side(0, core)
    finish(0)
    for s in range(per):
        local_w[s].wait()
    for s in range(per):
        w_copy(s, 1 - c).wait_recv()

    along = [s for s in range(ns) if along_y(s)]
    across = [s for s in range(ns) if not along_y(s)]
    finished = [(i, s) for i in range(nx) for s in along + across]
    count = [0]

    def advance(i, s):
        second(i, s)
        count[0] += 1
        if count[0] > LAG:
            third(*finished[count[0] - 1 - LAG])
        if count[0] > LAST:
            fourth(*finished[count[0] - 1 - LAST])

    for s in along:
        first(0, s)
    diagonal(ready, 2)
    earlier(1)
    finish(1)
    for s in across:
        first(0, s)
    cut = (len(along) + 1) // 2
    for s in along[:cut] + across:
        advance(0, s)
    for i in range(1, nx):
        landed(0, i)
        for s in along:
            first(i, s)
        for s in (across if i > 1 else []) + along[cut:]:
            advance(i - 1, s)
        landed(1, i)
        for s in across:
            first(i, s)
        for s in along[:cut]:
            advance(i, s)
    for s in across + along[cut:]:
        advance(nx - 1, s)
    for chunk in finished[-LAG:]:
        third(*chunk)
    for chunk in finished[-LAST:]:
        fourth(*chunk)

    @pl.when(c == 0)
    def _():
        for n, (buf, own) in enumerate(kv):
            kv_copy(buf, own, n, b, partner, kv_send.at[n, nx]).wait_send()

    for j in range(1, nx):
        @pl.when(j > x)
        def _():
            for n, (buf, own) in enumerate(kv):
                kv_copy(buf, own, n, b, j * 2 + c, kv_send.at[n, j]).wait_send()

    for j in range(nx - 1):
        @pl.when(j < x)
        def _():
            for n, (buf, own) in enumerate(kv):
                at = j * 2 + c
                kv_copy(buf, buf.at[at], n, at, partner, relay_send.at[n, j]).wait_send()

    for s in range(per):
        w_copy(s, c).wait_send()
    for g in range(2):
        for i in range(1, nx):
            att_copy(g, i, x).wait_send()

    for i in range(nx):
        for s in range(ns):
            y_copy(i, s).wait_send()
            p_copy(i, s).wait_send()
            z_each(i, lambda m: z_copy(i, s, m).wait_send())


def shards(nb, nh, queries, key_rows, value_head_rows, out_weight):
    rows, qcols = queries.shape
    depth, wcols = out_weight.shape
    heads = qcols // HEAD_SIZE
    nx, nz = nb // 2, nh // 2
    pairs = nz // 2
    piece, half, quarter = rows // nh, rows // 2, rows // 4
    step = math.gcd(wcols, COLUMN_STEP)
    ns = 2 * wcols // step
    tile = math.gcd(rows, KEY_TILE)
    q = queries.reshape(pairs, 2, 2, piece, qcols)
    dma = pltpu.SemaphoreType.DMA
    vmem = pl.BlockSpec(memory_space=pltpu.VMEM)
    hbm = pl.BlockSpec(memory_space=pl.ANY)
    return pl.pallas_call(
        functools.partial(kernel, nb, nh),
        out_shape=jax.ShapeDtypeStruct((piece, wcols * nb), BF16),
        in_specs=[hbm, hbm, hbm, hbm],
        out_specs=vmem,
        scratch_shapes=[
            pltpu.VMEM((2, 2, pairs, piece, qcols), BF16),
            pltpu.VMEM((nb, rows, HEAD_SIZE), BF16),
            pltpu.VMEM((nb, rows, HEAD_SIZE), BF16),
            pltpu.VMEM((nb, HEAD_SIZE + TOTAL_ROWS, rows), BF16),
            pltpu.VMEM((ns, depth, step), BF16),
            pltpu.VMEM((2, rows // tile, tile, half), F32),
            pltpu.VMEM((2, 8, half), F32),
            pltpu.VMEM((2, heads, HEAD_SIZE + TOTAL_ROWS, half), F32),
            pltpu.VMEM((2, heads, 8, half), F32),
            pltpu.VMEM((nx, 2, 2, quarter, qcols), BF16),
            pltpu.VMEM((nx, ns, half, step), BF16),
            pltpu.VMEM((nx, ns, half, step), BF16),
            pltpu.VMEM((nx, ns, quarter, step), BF16),
            pltpu.VMEM((nx, ns, quarter, step), BF16),
            pltpu.VMEM((nx, ns, quarter, step), F32),
            pltpu.VMEM((nx, ns, pairs, piece, step), BF16),
            pltpu.VMEM((nx, ns, pairs, piece, step), BF16),
            dma((6 + ns // 2,)),
            dma((2, nx + 1)),
            dma((2, nb)),
            dma((2, nx)),
            dma((ns // 2,)),
            dma((ns // 2,)),
            dma((2, nx)),
            dma((2, nx)),
            dma((nx, ns)),
            dma((nx, ns)),
            dma((nx, ns)),
            dma((nx, ns)),
            dma((nx, ns, pairs)),
            dma((nx, ns, pairs)),
        ],
        compiler_params=pltpu.CompilerParams(
            collective_id=0, has_side_effects=True, vmem_limit_bytes=66_000_000),
    )(q, key_rows, value_head_rows, out_weight)


def solution(mesh):
    in_specs = (P("blk", "heads"), P("blk", None), P("blk", None), P("heads", "blk"))
    out_specs = P(("blk", "heads"), None)
    body = functools.partial(shards, mesh.shape["blk"], mesh.shape["heads"])
    return jax.shard_map(body, mesh=mesh, in_specs=in_specs, out_specs=out_specs, check_vma=False)
```

```python
import functools
import math

import jax
import jax.numpy as jnp
from jax import lax
from jax.experimental import pallas as pl
from jax.experimental.pallas import tpu as pltpu
from jax.sharding import PartitionSpec as P

QUERY_HEADS = 64
KEY_VALUE_HEADS = 8
HEAD_SIZE = 128
MASKED_SCORE = -1e30
COLUMN_STEP = 256
TOTAL_ROWS = 16
LAG = 4
LAST = 9
KEY_TILE = 256
F32 = jnp.float32
BF16 = jnp.bfloat16


def kernel(nb, nh, q_hbm, k_ref, v_ref, w_ref, out_ref,
           q_ref, kbuf, vbuf, vturn, wbuf, sbuf, mbuf, acc, top, att, ysend, yrecv, psend, precv, kept, zsend, zrecv,
           local_sem, kv_send, kv_recv, relay_send, w_send, w_recv,
           att_send, att_recv, y_send, y_recv, p_send, p_recv, z_send, z_recv):
    nx, nz = nb // 2, nh // 2
    rows = k_ref.shape[0]
    piece = rows // nh
    half, quarter = rows // 2, rows // 4
    pairs = nz // 2
    heads = q_ref.shape[4] // HEAD_SIZE
    wcols = w_ref.shape[1]
    step = wbuf.shape[2]
    per = wcols // step
    ns = 2 * per
    scale = math.log2(math.e) * HEAD_SIZE ** (-0.5)

    b, h = lax.axis_index("blk"), lax.axis_index("heads")
    x, c = b // 2, b % 2
    z, y = h // 2, h % 2
    odd, seat = z % 2, z // 2
    partner = x * 2 + (1 - c)
    kv_col = pl.multiple_of((h * heads // (QUERY_HEADS // KEY_VALUE_HEADS)) * HEAD_SIZE, HEAD_SIZE)

    def remote(src, dst, ssem, rsem, blk, hd):
        return pltpu.make_async_remote_copy(
            src_ref=src, dst_ref=dst, send_sem=ssem, recv_sem=rsem,
            device_id=(blk, hd), device_id_type=pl.DeviceIdType.MESH)

    k_own = k_ref.at[:, pl.ds(kv_col, HEAD_SIZE)]
    v_own = v_ref.at[:, pl.ds(kv_col, HEAD_SIZE)]
    local_k = pltpu.make_async_copy(k_own, kbuf.at[b], local_sem.at[0])
    local_v = pltpu.make_async_copy(v_own, vbuf.at[b], local_sem.at[1])
    local_k.start()
    local_v.start()

    def group_y(g):
        return jnp.where(g == 0, 1 - y, y)

    def group_odd(u):
        return (1 - odd) if u == 0 else odd

    local_q = [pltpu.make_async_copy(q_hbm.at[:, group_odd(u), group_y(g)], q_ref.at[g, u], local_sem.at[2 + 2 * g + u])
               for g in range(2) for u in range(2)]
    for copy in local_q:
        copy.start()

    def w_cols(s):
        return w_ref.at[:, pl.ds(s * step, step)]

    local_w = [pltpu.make_async_copy(w_cols(s), wbuf.at[c * per + s], local_sem.at[6 + s]) for s in range(per)]
    for copy in local_w:
        copy.start()

    barrier = pltpu.get_barrier_semaphore()

    def greet(blk, hd):
        pl.semaphore_signal(barrier, inc=1, device_id=(blk, hd), device_id_type=pl.DeviceIdType.MESH)

    z_pair = (z + 1 - 2 * odd) * 2 + y
    y_pair = z * 2 + (1 - y)

    def owner(m):
        return (2 * m + odd) * 2 + y

    greet(partner, h)
    greet(b, y_pair)
    greet(b, z_pair)
    for j in range(nx):
        for m in range(pairs):
            @pl.when(jnp.logical_or(j != x, m != seat))
            def _():
                greet(j * 2 + c, owner(m))
    pl.semaphore_wait(barrier, 3 + nx * pairs - 1)

    kv = ((kbuf, k_own), (vbuf, v_own))

    def kv_copy(buf, own, n, src_blk, dst_blk, ssem):
        return remote(own, buf.at[src_blk], ssem, kv_recv.at[n, src_blk], dst_blk, h)

    @pl.when(c == 0)
    def _():
        for n, (buf, own) in enumerate(kv):
            kv_copy(buf, own, n, b, partner, kv_send.at[n, nx]).start()

    def kv_forward():
        for j in range(1, nx):
            @pl.when(j > x)
            def _():
                for n, (buf, own) in enumerate(kv):
                    kv_copy(buf, own, n, b, j * 2 + c, kv_send.at[n, j]).start()

    kv_forward()

    def w_copy(s, side):
        return remote(w_cols(s), wbuf.at[side * per + s], w_send.at[s], w_recv.at[s], partner, h)

    for s in range(per):
        w_copy(s, c).start()

    def turn(j):
        vturn[j, :HEAD_SIZE] = vbuf[j].T
        vturn[j, HEAD_SIZE:] = jnp.ones((TOTAL_ROWS, rows), BF16)

    tile = sbuf.shape[2]
    tiles = rows // tile

    def score_tile(g, hd, j, t, own):
        cols = pl.ds(pl.multiple_of(hd * HEAD_SIZE, HEAD_SIZE), HEAD_SIZE)
        q = q_ref[g, :, :, :, cols].reshape(half, HEAD_SIZE)
        k = kbuf[j, t * tile:(t + 1) * tile]
        s = lax.dot_general(k, q, (((1,), (1,)), ((), ())), preferred_element_type=F32) * scale
        if own:
            row = lax.broadcasted_iota(jnp.int32, (tile, half), 1)
            chip = row % quarter // piece * 2 + jnp.where(row < quarter, 1 - odd, odd)
            position = (chip * 2 + group_y(g)) * piece + row % piece
            visible = position >= lax.broadcasted_iota(jnp.int32, (tile, half), 0) + t * tile
            s = jnp.where(visible, s, MASKED_SCORE)
        return s

    def block(g, j, own):
        def put(hd, slot, t, m):
            s = score_tile(g, hd, j, t, own)
            sbuf[slot, t] = s
            n = jnp.max(s, axis=0, keepdims=True)
            return n if m is None else jnp.maximum(m, n)

        def step(hd, following, slot):
            m = mbuf[slot][:1]
            if not own:
                old = top[g, hd][:1]
                m = jnp.maximum(old, m)
            mixed, ahead = None, None
            for t in range(tiles):
                ahead = put(following, 1 - slot, t, ahead)
                p = jnp.exp2(sbuf[slot, t] - m).astype(BF16)
                d = jnp.dot(vturn[j, :, t * tile:(t + 1) * tile], p, preferred_element_type=F32)
                mixed = d if mixed is None else mixed + d
            mbuf[1 - slot] = jnp.broadcast_to(ahead, (8, half))
            if not own:
                mixed += acc[g, hd] * jnp.exp2(old - m)
            acc[g, hd] = mixed
            top[g, hd] = jnp.broadcast_to(m, (8, half))

        ahead = None
        for t in range(tiles):
            ahead = put(0, 0, t, ahead)
        mbuf[0] = jnp.broadcast_to(ahead, (8, half))

        def pair(i, carry):
            step(2 * i, 2 * i + 1, 0)
            step(2 * i + 1, jnp.minimum(2 * i + 2, heads - 1), 1)
            return carry

        lax.fori_loop(0, heads // 2, pair, 0, unroll=True)

    def side(g, core):
        def one(i, carry):
            block(g, 2 * (x - 1 - i) + core, False)
            return carry

        lax.fori_loop(0, x, one, 0)

    def earlier(g):
        def one(i, carry):
            block(g, b - 1 - i, False)
            return carry

        lax.fori_loop(0, b, one, 0)

    def diagonal(start, stop):
        def one(g, carry):
            block(g, b, True)
            return carry

        lax.fori_loop(start, stop, one, 0)

    def att_copy(g, i, src):
        return remote(att.at[src, g], att.at[src, g], att_send.at[g, i], att_recv.at[g, src],
                      lax.rem(x + i, nx) * 2 + c, h)

    def finish(g):
        def one(hd, carry):
            cols = pl.ds(pl.multiple_of(hd * HEAD_SIZE, HEAD_SIZE), HEAD_SIZE)
            a = acc[g, hd]
            mixed = (a[:HEAD_SIZE] / a[HEAD_SIZE:HEAD_SIZE + 1]).T.astype(BF16)
            att[x, g, :, :, cols] = mixed.reshape(2, quarter, HEAD_SIZE)
            return carry

        lax.fori_loop(0, heads, one, 0, unroll=True)
        for i in range(1, nx):
            att_copy(g, i, x).start()

    def wait_partner():
        @pl.when(c == 1)
        def _():
            for n, (buf, own) in enumerate(kv):
                kv_copy(buf, own, n, b - 1, partner, kv_send.at[n, nx]).wait_recv()
            turn(b - 1)

    def arrive(core):
        for j in range(nx - 1):
            @pl.when(j < x)
            def _():
                at = j * 2 + core
                for n, (buf, own) in enumerate(kv):
                    kv_copy(buf, own, n, at, partner, kv_send.at[n, 0]).wait_recv()

                @pl.when(c == core)
                def _():
                    for n, (buf, own) in enumerate(kv):
                        kv_copy(buf, buf.at[at], n, at, partner, relay_send.at[n, j]).start()

                turn(at)

    def chip(i):
        return x if i == 0 else lax.rem(x + i, nx)

    def along_y(s):
        return s < ns - ns // 4

    def y_copy(i, s):
        return remote(ysend.at[i, s], yrecv.at[i, s], y_send.at[i, s], y_recv.at[i, s], b, y_pair if along_y(s) else z_pair)

    def p_copy(i, s):
        return remote(psend.at[i, s], precv.at[i, s], p_send.at[i, s], p_recv.at[i, s], b, z_pair if along_y(s) else y_pair)

    def z_copy(i, s, m):
        return remote(zsend.at[i, s, m], zrecv.at[x, s, seat], z_send.at[i, s, m], z_recv.at[x, s, seat],
                      chip(i) * 2 + c, owner(m))

    def z_each(i, body):
        for m in range(pairs):
            if i == 0:
                pl.when(m != seat)(functools.partial(body, m))
            else:
                body(m)

    def project(i, s, far):
        a = att[chip(i), far] if along_y(s) else att[chip(i), :, far]
        return jnp.dot(a.reshape(half, a.shape[-1]), wbuf[s], preferred_element_type=F32)

    def first(i, s):
        ysend[i, s] = project(i, s, 0).astype(BF16)
        y_copy(i, s).start()

    def second(i, s):
        d = project(i, s, 1)
        y_copy(i, s).wait_recv()
        d += yrecv[i, s].astype(F32)
        psend[i, s] = d[:quarter].astype(BF16)
        p_copy(i, s).start()
        kept[i, s] = d[quarter:]

    def third(i, s):
        p_copy(i, s).wait_recv()
        d = (kept[i, s] + precv[i, s].astype(F32)).astype(BF16)
        zsend[i, s] = d.reshape(pairs, piece, step)
        z_each(i, lambda m: z_copy(i, s, m).start())
        if i == 0:
            zrecv[x, s, seat] = zsend[i, s, seat]

    def fourth(i, s):
        src = x if i == 0 else lax.rem(x + nx - i, nx)

        def arrived(m):
            remote(zsend.at[0, s, m], zrecv.at[src, s, m], z_send.at[0, s, m], z_recv.at[src, s, m], b, y_pair).wait_recv()

        z_each(i, arrived)
        total = zrecv[src, s, 0].astype(F32)
        for m in range(1, pairs):
            total += zrecv[src, s, m].astype(F32)
        col = pl.multiple_of((src * ns + s) * step, step)
        out_ref[:, pl.ds(col, step)] = total.astype(BF16)

    def landed(g, i):
        att_copy(g, i, chip(i)).wait_recv()

    local_k.wait()
    local_v.wait()
    turn(b)
    for copy in local_q:
        copy.wait()
    ready = jnp.where(jnp.logical_and(x > 0, c == 0), 2, 1)
    diagonal(0, ready)
    wait_partner()

    @pl.when(c == 1)
    def _():
        block(0, b - 1, False)

    for core in (1, 0):
        arrive(core)
        side(0, core)
    finish(0)
    for s in range(per):
        local_w[s].wait()
    for s in range(per):
        w_copy(s, 1 - c).wait_recv()

    along = [s for s in range(ns) if along_y(s)]
    across = [s for s in range(ns) if not along_y(s)]
    finished = [(i, s) for i in range(nx) for s in along + across]
    count = [0]

    def advance(i, s):
        second(i, s)
        count[0] += 1
        if count[0] > LAG:
            third(*finished[count[0] - 1 - LAG])
        if count[0] > LAST:
            fourth(*finished[count[0] - 1 - LAST])

    for s in along:
        first(0, s)
    diagonal(ready, 2)
    earlier(1)
    finish(1)
    for s in across:
        first(0, s)
    cut = (len(along) + 1) // 2
    for s in along[:cut] + across:
        advance(0, s)
    for i in range(1, nx):
        landed(0, i)
        for s in along:
            first(i, s)
        for s in (across if i > 1 else []) + along[cut:]:
            advance(i - 1, s)
        landed(1, i)
        for s in across:
            first(i, s)
        for s in along[:cut]:
            advance(i, s)
    for s in across + along[cut:]:
        advance(nx - 1, s)
    for chunk in finished[-LAG:]:
        third(*chunk)
    for chunk in finished[-LAST:]:
        fourth(*chunk)

    @pl.when(c == 0)
    def _():
        for n, (buf, own) in enumerate(kv):
            kv_copy(buf, own, n, b, partner, kv_send.at[n, nx]).wait_send()

    for j in range(1, nx):
        @pl.when(j > x)
        def _():
            for n, (buf, own) in enumerate(kv):
                kv_copy(buf, own, n, b, j * 2 + c, kv_send.at[n, j]).wait_send()

    for j in range(nx - 1):
        @pl.when(j < x)
        def _():
            for n, (buf, own) in enumerate(kv):
                at = j * 2 + c
                kv_copy(buf, buf.at[at], n, at, partner, relay_send.at[n, j]).wait_send()

    for s in range(per):
        w_copy(s, c).wait_send()
    for g in range(2):
        for i in range(1, nx):
            att_copy(g, i, x).wait_send()

    for i in range(nx):
        for s in range(ns):
            y_copy(i, s).wait_send()
            p_copy(i, s).wait_send()
            z_each(i, lambda m: z_copy(i, s, m).wait_send())


def shards(nb, nh, queries, key_rows, value_head_rows, out_weight):
    rows, qcols = queries.shape
    depth, wcols = out_weight.shape
    heads = qcols // HEAD_SIZE
    nx, nz = nb // 2, nh // 2
    pairs = nz // 2
    piece, half, quarter = rows // nh, rows // 2, rows // 4
    step = math.gcd(wcols, COLUMN_STEP)
    ns = 2 * wcols // step
    tile = math.gcd(rows, KEY_TILE)
    q = queries.reshape(pairs, 2, 2, piece, qcols)
    dma = pltpu.SemaphoreType.DMA
    vmem = pl.BlockSpec(memory_space=pltpu.VMEM)
    hbm = pl.BlockSpec(memory_space=pl.ANY)
    return pl.pallas_call(
        functools.partial(kernel, nb, nh),
        out_shape=jax.ShapeDtypeStruct((piece, wcols * nb), BF16),
        in_specs=[hbm, hbm, hbm, hbm],
        out_specs=vmem,
        scratch_shapes=[
            pltpu.VMEM((2, 2, pairs, piece, qcols), BF16),
            pltpu.VMEM((nb, rows, HEAD_SIZE), BF16),
            pltpu.VMEM((nb, rows, HEAD_SIZE), BF16),
            pltpu.VMEM((nb, HEAD_SIZE + TOTAL_ROWS, rows), BF16),
            pltpu.VMEM((ns, depth, step), BF16),
            pltpu.VMEM((2, rows // tile, tile, half), F32),
            pltpu.VMEM((2, 8, half), F32),
            pltpu.VMEM((2, heads, HEAD_SIZE + TOTAL_ROWS, half), F32),
            pltpu.VMEM((2, heads, 8, half), F32),
            pltpu.VMEM((nx, 2, 2, quarter, qcols), BF16),
            pltpu.VMEM((nx, ns, half, step), BF16),
            pltpu.VMEM((nx, ns, half, step), BF16),
            pltpu.VMEM((nx, ns, quarter, step), BF16),
            pltpu.VMEM((nx, ns, quarter, step), BF16),
            pltpu.VMEM((nx, ns, quarter, step), F32),
            pltpu.VMEM((nx, ns, pairs, piece, step), BF16),
            pltpu.VMEM((nx, ns, pairs, piece, step), BF16),
            dma((6 + ns // 2,)),
            dma((2, nx + 1)),
            dma((2, nb)),
            dma((2, nx)),
            dma((ns // 2,)),
            dma((ns // 2,)),
            dma((2, nx)),
            dma((2, nx)),
            dma((nx, ns)),
            dma((nx, ns)),
            dma((nx, ns)),
            dma((nx, ns)),
            dma((nx, ns, pairs)),
            dma((nx, ns, pairs)),
        ],
        compiler_params=pltpu.CompilerParams(
            collective_id=0, has_side_effects=True, vmem_limit_bytes=66_000_000),
    )(q, key_rows, value_head_rows, out_weight)


def solution(mesh):
    in_specs = (P("blk", "heads"), P("blk", None), P("blk", None), P("heads", "blk"))
    out_specs = P(("blk", "heads"), None)
    body = functools.partial(shards, mesh.shape["blk"], mesh.shape["heads"])
    return jax.shard_map(body, mesh=mesh, in_specs=in_specs, out_specs=out_specs, check_vma=False)
```

```python
import functools
import math

import jax
import jax.numpy as jnp
from jax import lax
from jax.experimental import pallas as pl
from jax.experimental.pallas import tpu as pltpu
from jax.sharding import PartitionSpec as P

QUERY_HEADS = 64
KEY_VALUE_HEADS = 8
HEAD_SIZE = 128
MASKED_SCORE = -1e30
COLUMN_STEP = 256
TOTAL_ROWS = 16
LAG = 4
LAST = 9
KEY_TILE = 256
F32 = jnp.float32
BF16 = jnp.bfloat16


def kernel(nb, nh, q_hbm, k_ref, v_ref, w_ref, out_ref,
           q_ref, kbuf, vbuf, vturn, wbuf, sbuf, mbuf, acc, top, att, ysend, yrecv, psend, precv, kept, zsend, zrecv,
           local_sem, kv_send, kv_recv, relay_send, w_send, w_recv,
           att_send, att_recv, y_send, y_recv, p_send, p_recv, z_send, z_recv):
    nx, nz = nb // 2, nh // 2
    rows = k_ref.shape[0]
    piece = rows // nh
    half, quarter = rows // 2, rows // 4
    pairs = nz // 2
    heads = q_ref.shape[4] // HEAD_SIZE
    wcols = w_ref.shape[1]
    step = wbuf.shape[2]
    per = wcols // step
    ns = 2 * per
    scale = math.log2(math.e) * HEAD_SIZE ** (-0.5)

    b, h = lax.axis_index("blk"), lax.axis_index("heads")
    x, c = b // 2, b % 2
    z, y = h // 2, h % 2
    odd, seat = z % 2, z // 2
    partner = x * 2 + (1 - c)
    kv_col = pl.multiple_of((h * heads // (QUERY_HEADS // KEY_VALUE_HEADS)) * HEAD_SIZE, HEAD_SIZE)

    def remote(src, dst, ssem, rsem, blk, hd):
        return pltpu.make_async_remote_copy(
            src_ref=src, dst_ref=dst, send_sem=ssem, recv_sem=rsem,
            device_id=(blk, hd), device_id_type=pl.DeviceIdType.MESH)

    k_own = k_ref.at[:, pl.ds(kv_col, HEAD_SIZE)]
    v_own = v_ref.at[:, pl.ds(kv_col, HEAD_SIZE)]
    local_k = pltpu.make_async_copy(k_own, kbuf.at[b], local_sem.at[0])
    local_v = pltpu.make_async_copy(v_own, vbuf.at[b], local_sem.at[1])
    local_k.start()
    local_v.start()

    def group_y(g):
        return jnp.where(g == 0, 1 - y, y)

    def group_odd(u):
        return (1 - odd) if u == 0 else odd

    local_q = [pltpu.make_async_copy(q_hbm.at[:, group_odd(u), group_y(g)], q_ref.at[g, u], local_sem.at[2 + 2 * g + u])
               for g in range(2) for u in range(2)]
    for copy in local_q:
        copy.start()

    def w_cols(s):
        return w_ref.at[:, pl.ds(s * step, step)]

    local_w = [pltpu.make_async_copy(w_cols(s), wbuf.at[c * per + s], local_sem.at[6 + s]) for s in range(per)]
    for copy in local_w:
        copy.start()

    barrier = pltpu.get_barrier_semaphore()

    def greet(blk, hd):
        pl.semaphore_signal(barrier, inc=1, device_id=(blk, hd), device_id_type=pl.DeviceIdType.MESH)

    z_pair = (z + 1 - 2 * odd) * 2 + y
    y_pair = z * 2 + (1 - y)

    def owner(m):
        return (2 * m + odd) * 2 + y

    greet(partner, h)
    greet(b, y_pair)
    greet(b, z_pair)
    for j in range(nx):
        for m in range(pairs):
            @pl.when(jnp.logical_or(j != x, m != seat))
            def _():
                greet(j * 2 + c, owner(m))
    pl.semaphore_wait(barrier, 3 + nx * pairs - 1)

    kv = ((kbuf, k_own), (vbuf, v_own))

    def kv_copy(buf, own, n, src_blk, dst_blk, ssem):
        return remote(own, buf.at[src_blk], ssem, kv_recv.at[n, src_blk], dst_blk, h)

    @pl.when(c == 0)
    def _():
        for n, (buf, own) in enumerate(kv):
            kv_copy(buf, own, n, b, partner, kv_send.at[n, nx]).start()

    def kv_forward():
        for j in range(1, nx):
            @pl.when(j > x)
            def _():
                for n, (buf, own) in enumerate(kv):
                    kv_copy(buf, own, n, b, j * 2 + c, kv_send.at[n, j]).start()

    kv_forward()

    def w_copy(s, side):
        return remote(w_cols(s), wbuf.at[side * per + s], w_send.at[s], w_recv.at[s], partner, h)

    for s in range(per):
        w_copy(s, c).start()

    def turn(j):
        vturn[j, :HEAD_SIZE] = vbuf[j].T
        vturn[j, HEAD_SIZE:] = jnp.ones((TOTAL_ROWS, rows), BF16)

    tile = sbuf.shape[2]
    tiles = rows // tile

    def score_tile(g, hd, j, t, own):
        cols = pl.ds(pl.multiple_of(hd * HEAD_SIZE, HEAD_SIZE), HEAD_SIZE)
        q = q_ref[g, :, :, :, cols].reshape(half, HEAD_SIZE)
        k = kbuf[j, t * tile:(t + 1) * tile]
        s = lax.dot_general(k, q, (((1,), (1,)), ((), ())), preferred_element_type=F32) * scale
        if own:
            row = lax.broadcasted_iota(jnp.int32, (tile, half), 1)
            chip = row % quarter // piece * 2 + jnp.where(row < quarter, 1 - odd, odd)
            position = (chip * 2 + group_y(g)) * piece + row % piece
            visible = position >= lax.broadcasted_iota(jnp.int32, (tile, half), 0) + t * tile
            s = jnp.where(visible, s, MASKED_SCORE)
        return s

    def block(g, j, own):
        def put(hd, slot, t, m):
            s = score_tile(g, hd, j, t, own)
            sbuf[slot, t] = s
            n = jnp.max(s, axis=0, keepdims=True)
            return n if m is None else jnp.maximum(m, n)

        def step(hd, following, slot):
            m = mbuf[slot][:1]
            if not own:
                old = top[g, hd][:1]
                m = jnp.maximum(old, m)
            mixed, ahead = None, None
            for t in range(tiles):
                ahead = put(following, 1 - slot, t, ahead)
                p = jnp.exp2(sbuf[slot, t] - m).astype(BF16)
                d = jnp.dot(vturn[j, :, t * tile:(t + 1) * tile], p, preferred_element_type=F32)
                mixed = d if mixed is None else mixed + d
            mbuf[1 - slot] = jnp.broadcast_to(ahead, (8, half))
            if not own:
                mixed += acc[g, hd] * jnp.exp2(old - m)
            acc[g, hd] = mixed
            top[g, hd] = jnp.broadcast_to(m, (8, half))

        ahead = None
        for t in range(tiles):
            ahead = put(0, 0, t, ahead)
        mbuf[0] = jnp.broadcast_to(ahead, (8, half))

        def pair(i, carry):
            step(2 * i, 2 * i + 1, 0)
            step(2 * i + 1, jnp.minimum(2 * i + 2, heads - 1), 1)
            return carry

        lax.fori_loop(0, heads // 2, pair, 0, unroll=True)

    def side(g, core):
        def one(i, carry):
            block(g, 2 * (x - 1 - i) + core, False)
            return carry

        lax.fori_loop(0, x, one, 0)

    def earlier(g):
        def one(i, carry):
            block(g, b - 1 - i, False)
            return carry

        lax.fori_loop(0, b, one, 0)

    def diagonal(start, stop):
        def one(g, carry):
            block(g, b, True)
            return carry

        lax.fori_loop(start, stop, one, 0)

    def att_copy(g, i, src):
        return remote(att.at[src, g], att.at[src, g], att_send.at[g, i], att_recv.at[g, src],
                      lax.rem(x + i, nx) * 2 + c, h)

    def finish(g):
        def one(hd, carry):
            cols = pl.ds(pl.multiple_of(hd * HEAD_SIZE, HEAD_SIZE), HEAD_SIZE)
            a = acc[g, hd]
            mixed = (a[:HEAD_SIZE] / a[HEAD_SIZE:HEAD_SIZE + 1]).T.astype(BF16)
            att[x, g, :, :, cols] = mixed.reshape(2, quarter, HEAD_SIZE)
            return carry

        lax.fori_loop(0, heads, one, 0, unroll=True)
        for i in range(1, nx):
            att_copy(g, i, x).start()

    def wait_partner():
        @pl.when(c == 1)
        def _():
            for n, (buf, own) in enumerate(kv):
                kv_copy(buf, own, n, b - 1, partner, kv_send.at[n, nx]).wait_recv()
            turn(b - 1)

    def arrive(core):
        for j in range(nx - 1):
            @pl.when(j < x)
            def _():
                at = j * 2 + core
                for n, (buf, own) in enumerate(kv):
                    kv_copy(buf, own, n, at, partner, kv_send.at[n, 0]).wait_recv()

                @pl.when(c == core)
                def _():
                    for n, (buf, own) in enumerate(kv):
                        kv_copy(buf, buf.at[at], n, at, partner, relay_send.at[n, j]).start()

                turn(at)

    def chip(i):
        return x if i == 0 else lax.rem(x + i, nx)

    def along_y(s):
        return s < ns - ns // 4

    def y_copy(i, s):
        return remote(ysend.at[i, s], yrecv.at[i, s], y_send.at[i, s], y_recv.at[i, s], b, y_pair if along_y(s) else z_pair)

    def p_copy(i, s):
        return remote(psend.at[i, s], precv.at[i, s], p_send.at[i, s], p_recv.at[i, s], b, z_pair if along_y(s) else y_pair)

    def z_copy(i, s, m):
        return remote(zsend.at[i, s, m], zrecv.at[x, s, seat], z_send.at[i, s, m], z_recv.at[x, s, seat],
                      chip(i) * 2 + c, owner(m))

    def z_each(i, body):
        for m in range(pairs):
            if i == 0:
                pl.when(m != seat)(functools.partial(body, m))
            else:
                body(m)

    def project(i, s, far):
        a = att[chip(i), far] if along_y(s) else att[chip(i), :, far]
        return jnp.dot(a.reshape(half, a.shape[-1]), wbuf[s], preferred_element_type=F32)

    def first(i, s):
        ysend[i, s] = project(i, s, 0).astype(BF16)
        y_copy(i, s).start()

    def second(i, s):
        d = project(i, s, 1)
        y_copy(i, s).wait_recv()
        d += yrecv[i, s].astype(F32)
        psend[i, s] = d[:quarter].astype(BF16)
        p_copy(i, s).start()
        kept[i, s] = d[quarter:]

    def third(i, s):
        p_copy(i, s).wait_recv()
        d = (kept[i, s] + precv[i, s].astype(F32)).astype(BF16)
        zsend[i, s] = d.reshape(pairs, piece, step)
        z_each(i, lambda m: z_copy(i, s, m).start())
        if i == 0:
            zrecv[x, s, seat] = zsend[i, s, seat]

    def fourth(i, s):
        src = x if i == 0 else lax.rem(x + nx - i, nx)

        def arrived(m):
            remote(zsend.at[0, s, m], zrecv.at[src, s, m], z_send.at[0, s, m], z_recv.at[src, s, m], b, y_pair).wait_recv()

        z_each(i, arrived)
        total = zrecv[src, s, 0].astype(F32)
        for m in range(1, pairs):
            total += zrecv[src, s, m].astype(F32)
        col = pl.multiple_of((src * ns + s) * step, step)
        out_ref[:, pl.ds(col, step)] = total.astype(BF16)

    def landed(g, i):
        att_copy(g, i, chip(i)).wait_recv()

    local_k.wait()
    local_v.wait()
    turn(b)
    for copy in local_q:
        copy.wait()
    ready = jnp.where(jnp.logical_and(x > 0, c == 0), 2, 1)
    diagonal(0, ready)
    wait_partner()

    @pl.when(c == 1)
    def _():
        block(0, b - 1, False)

    for core in (1, 0):
        arrive(core)
        side(0, core)
    finish(0)
    for s in range(per):
        local_w[s].wait()
    for s in range(per):
        w_copy(s, 1 - c).wait_recv()

    along = [s for s in range(ns) if along_y(s)]
    across = [s for s in range(ns) if not along_y(s)]
    finished = [(i, s) for i in range(nx) for s in along + across]
    count = [0]

    def advance(i, s):
        second(i, s)
        count[0] += 1
        if count[0] > LAG:
            third(*finished[count[0] - 1 - LAG])
        if count[0] > LAST:
            fourth(*finished[count[0] - 1 - LAST])

    for s in along:
        first(0, s)
    diagonal(ready, 2)
    earlier(1)
    finish(1)
    for s in across:
        first(0, s)
    cut = (len(along) + 1) // 2
    for s in along[:cut] + across:
        advance(0, s)
    for i in range(1, nx):
        landed(0, i)
        for s in along:
            first(i, s)
            if s == along[cut - 1]:
                for t in (across if i > 1 else []) + along[cut:cut + 1]:
                    advance(i - 1, t)
        for s in along[cut + 1:]:
            advance(i - 1, s)
        landed(1, i)
        for s in across:
            first(i, s)
        for s in along[:cut]:
            advance(i, s)
    for s in across + along[cut:]:
        advance(nx - 1, s)
    for chunk in finished[-LAG:]:
        third(*chunk)
    for chunk in finished[-LAST:]:
        fourth(*chunk)

    @pl.when(c == 0)
    def _():
        for n, (buf, own) in enumerate(kv):
            kv_copy(buf, own, n, b, partner, kv_send.at[n, nx]).wait_send()

    for j in range(1, nx):
        @pl.when(j > x)
        def _():
            for n, (buf, own) in enumerate(kv):
                kv_copy(buf, own, n, b, j * 2 + c, kv_send.at[n, j]).wait_send()

    for j in range(nx - 1):
        @pl.when(j < x)
        def _():
            for n, (buf, own) in enumerate(kv):
                at = j * 2 + c
                kv_copy(buf, buf.at[at], n, at, partner, relay_send.at[n, j]).wait_send()

    for s in range(per):
        w_copy(s, c).wait_send()
    for g in range(2):
        for i in range(1, nx):
            att_copy(g, i, x).wait_send()

    for i in range(nx):
        for s in range(ns):
            y_copy(i, s).wait_send()
            p_copy(i, s).wait_send()
            z_each(i, lambda m: z_copy(i, s, m).wait_send())


def shards(nb, nh, queries, key_rows, value_head_rows, out_weight):
    rows, qcols = queries.shape
    depth, wcols = out_weight.shape
    heads = qcols // HEAD_SIZE
    nx, nz = nb // 2, nh // 2
    pairs = nz // 2
    piece, half, quarter = rows // nh, rows // 2, rows // 4
    step = math.gcd(wcols, COLUMN_STEP)
    ns = 2 * wcols // step
    tile = math.gcd(rows, KEY_TILE)
    q = queries.reshape(pairs, 2, 2, piece, qcols)
    dma = pltpu.SemaphoreType.DMA
    vmem = pl.BlockSpec(memory_space=pltpu.VMEM)
    hbm = pl.BlockSpec(memory_space=pl.ANY)
    return pl.pallas_call(
        functools.partial(kernel, nb, nh),
        out_shape=jax.ShapeDtypeStruct((piece, wcols * nb), BF16),
        in_specs=[hbm, hbm, hbm, hbm],
        out_specs=vmem,
        scratch_shapes=[
            pltpu.VMEM((2, 2, pairs, piece, qcols), BF16),
            pltpu.VMEM((nb, rows, HEAD_SIZE), BF16),
            pltpu.VMEM((nb, rows, HEAD_SIZE), BF16),
            pltpu.VMEM((nb, HEAD_SIZE + TOTAL_ROWS, rows), BF16),
            pltpu.VMEM((ns, depth, step), BF16),
            pltpu.VMEM((2, rows // tile, tile, half), F32),
            pltpu.VMEM((2, 8, half), F32),
            pltpu.VMEM((2, heads, HEAD_SIZE + TOTAL_ROWS, half), F32),
            pltpu.VMEM((2, heads, 8, half), F32),
            pltpu.VMEM((nx, 2, 2, quarter, qcols), BF16),
            pltpu.VMEM((nx, ns, half, step), BF16),
            pltpu.VMEM((nx, ns, half, step), BF16),
            pltpu.VMEM((nx, ns, quarter, step), BF16),
            pltpu.VMEM((nx, ns, quarter, step), BF16),
            pltpu.VMEM((nx, ns, quarter, step), F32),
            pltpu.VMEM((nx, ns, pairs, piece, step), BF16),
            pltpu.VMEM((nx, ns, pairs, piece, step), BF16),
            dma((6 + ns // 2,)),
            dma((2, nx + 1)),
            dma((2, nb)),
            dma((2, nx)),
            dma((ns // 2,)),
            dma((ns // 2,)),
            dma((2, nx)),
            dma((2, nx)),
            dma((nx, ns)),
            dma((nx, ns)),
            dma((nx, ns)),
            dma((nx, ns)),
            dma((nx, ns, pairs)),
            dma((nx, ns, pairs)),
        ],
        compiler_params=pltpu.CompilerParams(
            collective_id=0, has_side_effects=True, vmem_limit_bytes=66_000_000),
    )(q, key_rows, value_head_rows, out_weight)


def solution(mesh):
    in_specs = (P("blk", "heads"), P("blk", None), P("blk", None), P("heads", "blk"))
    out_specs = P(("blk", "heads"), None)
    body = functools.partial(shards, mesh.shape["blk"], mesh.shape["heads"])
    return jax.shard_map(body, mesh=mesh, in_specs=in_specs, out_specs=out_specs, check_vma=False)
```
